32 devices in a mesh: dp: 8 (over y, x, core), tensor: 4 (over z).
Axes of the slice: x: 2, y: 2, z: 4, core: 2. Of those that a mesh axis runs over, the one named last changes fastest.
Arguments:
- tokens: bfloat16 [4096, 1024], P('dp'), may hold values from -6 to 6
- segments: int32 [8, 512], P('dp'), may hold values from 0 to 1, never falling along the last dimension, each value on 1 to 384 neighbouring positions
- ln1_gain: float32 [1024], replicated, may hold values from 0.1 to 1.9
- ln1_bias: float32 [1024], replicated, may hold values from -3 to 3
- w_qkv: bfloat16 [1024, 3072], P(None, 'tensor'), may hold values from -0.2 to 0.2
- b_qv: float32 [16, 128], P('tensor'), may hold values from -3 to 3
- w_dense: bfloat16 [1024, 1024], P('tensor'), may hold values from -0.75 to 0.75
- b_dense: float32 [1024], replicated, may hold values from -3 to 3
- ln2_gain: float32 [1024], replicated, may hold values from 0.1 to 1.9
- ln2_bias: float32 [1024], replicated, may hold values from -3 to 3
- w_fc1: bfloat16 [1024, 4096], P(None, 'tensor'), may hold values from -0.1875 to 0.1875
- b_fc1: float32 [32, 128], P('tensor'), may hold values from -3 to 3
- w_fc2: bfloat16 [4096, 1024], P('tensor'), may hold values from -0.09375 to 0.09375
- b_fc2: float32 [1024], replicated, may hold values from -3 to 3
- cotangent: bfloat16 [4096, 1024], P('dp'), may hold values from -6 to 6
Outputs:
- block_out: bfloat16 [4096, 1024], P(('dp', 'tensor'))
- d_tokens: float32 [4096, 1024], P(('dp', 'tensor'))
- d_ln1_gain: float32 [1024], P(('dp', 'tensor'))
- d_ln1_bias: float32 [1024], P(('dp', 'tensor'))
- d_w_qkv: float32 [1024, 3072], P('dp', 'tensor')
- d_b_qv: float32 [16, 128], P('tensor', 'dp')
- d_w_dense: float32 [1024, 1024], P('tensor', 'dp')
- d_b_dense: float32 [1024], P(('dp', 'tensor'))
- d_ln2_gain: float32 [1024], P(('dp', 'tensor'))
- d_ln2_bias: float32 [1024], P(('dp', 'tensor'))
- d_w_fc1: float32 [1024, 4096], P('dp', 'tensor')
- d_b_fc1: float32 [32, 128], P('tensor', 'dp')
- d_w_fc2: float32 [4096, 1024], P('tensor', 'dp')
- d_b_fc2: float32 [1024], P(('dp', 'tensor'))
The draws below stay inside these ranges and needn't reach their ends.
Inputs may be any that keep to these rules, and one draw needn't show every extreme that they name: `segments`: along each row the numbers never fall; positions with equal numbers form one document of at most 384 tokens.
All inputs are finite; a program needn't handle non-finite values.
Results may differ from the reference program's by a relative error of at most 0.034.
The reference program's roundings to bfloat16 on the way count: a program that leaves them out, or rounds other values in their place, can miss the bound.
Values may be sent and summed in bfloat16 or wider, within the bound.
A program may use at most 128 MiB of HBM per device.

```python
import math
import jax
import jax.numpy as jnp
import numpy as np
from jax import lax

D = 1024
H = 16
HD = 64
FF = 4096
LEN = 512
ROWS = 8
TOKENS = 4096


def sign_pattern(key):
    bits = jax.random.randint(jax.random.fold_in(key, 7001), (D,), 0, 2)
    return (2 * bits - 1).astype(jnp.float32)


def draw_tokens(key, part):
    pattern = sign_pattern(key)
    key_noise, key_pick, key_lift, key_extra = jax.random.split(jax.random.fold_in(key, 7002), 4)
    share = max(1.0 / 32.0, 3.0 / LEN)
    picked = jax.random.bernoulli(key_pick, share, (TOKENS, 1))
    noise = jax.random.truncated_normal(key_noise, -6.0, 6.0, (TOKENS, D), jnp.float32)
    lift = jax.random.uniform(key_lift, (TOKENS, 1), jnp.float32, 2.5, 3.5)
    extra = 0.8 * jax.random.truncated_normal(key_extra, -3.0, 3.0, (TOKENS, D), jnp.float32)
    planted = lift * pattern[None, :] + extra
    return jnp.where(picked, planted, noise).astype(jnp.bfloat16)


def draw_w_qkv(key, part):
    pattern = sign_pattern(key)
    key_base, key_dir, key_rank = jax.random.split(jax.random.fold_in(key, 7003), 3)
    limit = min(6.0, 0.17 * math.sqrt(D))
    base = jax.random.truncated_normal(key_base, -limit, limit, (D, H, 3, HD), jnp.float32)
    base = base * (1.0 / math.sqrt(D))
    direction = (2 * jax.random.randint(key_dir, (H, HD), 0, 2) - 1).astype(jnp.float32) * (1.0 / math.sqrt(HD))
    boosted = max(2, H // 4)
    ranks = jax.random.permutation(key_rank, H)
    strength = jnp.where(ranks < boosted, 1.0 + 0.9 * ranks.astype(jnp.float32) / (boosted - 1), 0.0)
    along = pattern * (32.0 / D)
    lift = along[:, None, None] * (strength[:, None] * direction)[None, :, :]
    boost = jnp.stack([lift, lift, jnp.zeros_like(lift)], axis=2)
    return (base + boost).reshape(D, 3 * D).astype(jnp.bfloat16)


def raised(values, key, source, target, parts, factor):
    owner, partner = [(jnp.arange(values.shape[dim]) // (values.shape[dim] // parts)).reshape([-1 if axis == dim else 1 for axis in range(values.ndim)]) for dim in (source, target)]
    chosen = jax.random.permutation(key, parts)[partner]
    strong = (owner == chosen) | (owner == (partner + parts // 2) % parts)
    return jnp.where(strong, factor * values, values)


def shard_levels(key, extent, shards, smallest, largest):
    gain = 1.0
    for position, blocks in shards:
        draws = jax.random.uniform(jax.random.fold_in(jax.random.fold_in(key, 6), position), (blocks,), jnp.float32, smallest / len(shards), largest / len(shards))
        gain = gain * jnp.repeat(jnp.exp(draws), extent[position] // blocks).reshape((-1,) + (1,) * (len(extent) - 1 - position))
    return gain


def split_up(amount, total, most, slope):
    portions = [(1 << 20) // math.isqrt(rank ** slope) + 1 for rank in range(2, amount + 1)]
    spare, holding = total - most - (amount - 1), [1] * (amount - 1)
    while spare > 0:
        candidates = [i for i in range(amount - 1) if holding[i] < most]
        pool, remaining = sum([portions[i] for i in candidates]), spare
        for i in candidates:
            addition = min(most - holding[i], max(1, remaining * portions[i] // pool), spare)
            holding[i] = holding[i] + addition
            spare = spare - addition
    return np.array([most] + holding)


def uneven_parts(rng, amount, total, reach, lean):
    if amount == 2:
        one = jax.random.randint(rng, (), max(1, total - reach), min(reach, total - 1) + 1)
        return jnp.stack([one, total - one])
    tallies = jnp.asarray(split_up(amount, total, reach, lean), jnp.int32)
    twos = (amount - 1) // 2
    giver, taker = tallies[1:1 + 2 * twos:2], tallies[2:2 + 2 * twos:2]
    slack = jnp.minimum(giver - 1, reach - taker)
    passed = jax.random.randint(jax.random.fold_in(rng, 1), (twos,), 0, 1 << 20) % (slack + 1)
    tallies = tallies.at[1:1 + 2 * twos:2].set(giver - passed).at[2:2 + 2 * twos:2].set(taker + passed)
    return tallies[jax.random.permutation(jax.random.fold_in(rng, 2), amount)]


def gaussian(own_key, dims, deviation, bound, cuts=(), dtype=jnp.bfloat16):
    values = deviation * jax.random.normal(own_key, dims, jnp.float32)
    if cuts:
        values = values * shard_levels(own_key, dims, cuts, -0.22, 0.18)
    return jnp.clip(values, -bound, bound).astype(dtype)


def noise_with(key, dims, width, reach, cuts, heavy, kind=jnp.bfloat16):
    drawn = width * jax.random.normal(key, dims, jnp.float32)
    if cuts:
        drawn = drawn * shard_levels(key, dims, cuts, -0.22, 0.18)
    return jnp.clip(raised(drawn, jax.random.fold_in(key, 3), *heavy), -reach, reach).astype(kind)


def setup_inputs(seed: int = 0) -> dict:
    seeds = jax.random.split(jax.random.key(seed), 16)
    tokens = draw_tokens(jax.random.fold_in(seeds[15], 71), 0)
    segments = jax.vmap(lambda own: jnp.searchsorted(jnp.cumsum(uneven_parts(own, 2, LEN, LEN - LEN // 4, 0)), jnp.arange(LEN), side="right"))(jax.random.split(seeds[1], ROWS)).reshape((ROWS, LEN)).astype(jnp.int32)
    ln1_gain = jnp.clip(1.0 + 0.18 * jax.random.normal(seeds[2], (D,), jnp.float32), 0.1, 1.9)
    ln1_bias = gaussian(seeds[3], (D,), 0.5, 3.0, (), jnp.float32)
    w_qkv = draw_w_qkv(jax.random.fold_in(seeds[15], 71), 0)
    b_qv = gaussian(seeds[5], (H, 2 * HD), 0.5, 3.0, ((0, 4),), jnp.float32)
    w_dense = gaussian(seeds[6], (D, D), HD ** -0.5, 0.75, ((0, 4),))
    b_dense = gaussian(seeds[7], (D,), 0.5, 3.0, (), jnp.float32)
    ln2_gain = jnp.clip(1.0 + 0.18 * jax.random.normal(seeds[8], (D,), jnp.float32), 0.1, 1.9)
    ln2_bias = gaussian(seeds[9], (D,), 0.5, 3.0, (), jnp.float32)
    w_fc1 = gaussian(seeds[10], (D, FF), D ** -0.5, 0.1875, ((1, 4),))
    b_fc1 = gaussian(seeds[11], (FF // 128, 128), 0.5, 3.0, ((0, 4),), jnp.float32)
    w_fc2 = gaussian(seeds[12], (FF, D), FF ** -0.5, 0.09375, ((0, 4),))
    b_fc2 = gaussian(seeds[13], (D,), 0.5, 3.0, (), jnp.float32)
    cotangent = noise_with(seeds[14], (TOKENS, D), 1.0, 6.0, ((0, 8),), (0, 1, 8, 2.0))
    return {"tokens": tokens, "segments": segments, "ln1_gain": ln1_gain, "ln1_bias": ln1_bias, "w_qkv": w_qkv, "b_qv": b_qv, "w_dense": w_dense, "b_dense": b_dense, "ln2_gain": ln2_gain, "ln2_bias": ln2_bias, "w_fc1": w_fc1, "b_fc1": b_fc1, "w_fc2": w_fc2, "b_fc2": b_fc2, "cotangent": cotangent}


EPS = 1e-05
GELU_C = 0.7978845608028654
GELU_A = 0.044715
MASKED = -1e+30

def layer_norm(row_block, gain_row, shift_row):
    row_mean = lax.optimization_barrier(jnp.mean(row_block, axis=-1, keepdims=True))
    centred = row_block - row_mean
    row_var = lax.optimization_barrier(jnp.mean(centred * centred, axis=-1, keepdims=True))
    inv_std = lax.rsqrt(row_var + EPS)
    normed = centred * inv_std
    return (normed * gain_row + shift_row, normed, inv_std)

def norm_back(grad_rows, normed, inv_std, gain_row):
    grad_normed = grad_rows * gain_row
    mean_one = lax.optimization_barrier(jnp.mean(grad_normed, axis=-1, keepdims=True))
    mean_two = lax.optimization_barrier(jnp.mean(grad_normed * normed, axis=-1, keepdims=True))
    grad_in = inv_std * (grad_normed - mean_one - normed * mean_two)
    return (grad_in, lax.optimization_barrier(jnp.sum(grad_rows * normed, axis=0)), lax.optimization_barrier(jnp.sum(grad_rows, axis=0)))

def gelu_value(pre_act):
    tanh_val = jnp.tanh(GELU_C * (pre_act + GELU_A * pre_act * pre_act * pre_act))
    return 0.5 * pre_act * (1.0 + tanh_val)

def gelu_slope(pre_act):
    tanh_val = jnp.tanh(GELU_C * (pre_act + GELU_A * pre_act * pre_act * pre_act))
    return 0.5 * (1.0 + tanh_val) + 0.5 * pre_act * (1.0 - tanh_val * tanh_val) * GELU_C * (1.0 + 3.0 * GELU_A * pre_act * pre_act)

def alibi_slopes(head_ids, head_total):
    return jnp.power(2.0, -8.0 * (head_ids.astype(jnp.float32) + 1.0) / head_total)

def qkv_bias(bias_table):
    head_size = bias_table.shape[1] // 2
    zero_keys = jnp.zeros((bias_table.shape[0], head_size), jnp.float32)
    return jnp.concatenate([bias_table[:, :head_size], zero_keys, bias_table[:, head_size:]], axis=1).reshape(-1)

def cross_rows(left_mat, right_mat):
    return lax.dot_general(left_mat, right_mat, (((0,), (0,)), ((), ())), preferred_element_type=jnp.float32)

def dot_transposed(left_mat, right_mat):
    return lax.dot_general(left_mat, right_mat, (((1,), (1,)), ((), ())), preferred_element_type=jnp.float32)

def masked_scores(queries, keys_all, slopes, doc_ids):
    raw_dot = jnp.einsum('qhe,khe->hqk', queries.astype(jnp.float32), keys_all.astype(jnp.float32))
    places = jnp.arange(doc_ids.shape[0])
    distance = (places[:, None] - places[None, :]).astype(jnp.float32)
    allowed = jnp.logical_and(doc_ids[:, None] == doc_ids[None, :], places[None, :] <= places[:, None])
    scores = raw_dot * (1.0 / math.sqrt(HD)) - slopes[:, None, None] * distance[None]
    return jnp.where(allowed[None], scores, MASKED)

def row_pass(weights, tok_row, doc_ids, cot_row):
    ln1_gain, ln1_bias, w_qkv, b_qv, w_dense, b_dense, ln2_gain, ln2_bias, w_fc1, b_fc1, w_fc2, b_fc2 = weights
    length = tok_row.shape[0]
    tokens_f = tok_row.astype(jnp.float32)
    norm_one, normed_one, inv_one = layer_norm(tokens_f, ln1_gain, ln1_bias)
    input_one = norm_one.astype(jnp.bfloat16)
    qkv_rows = (jnp.dot(input_one, w_qkv, preferred_element_type=jnp.float32) + qkv_bias(b_qv)).astype(jnp.bfloat16)
    qkv_rows = qkv_rows.reshape(length, H, 3, HD)
    queries = qkv_rows[:, :, 0]
    keys_all = qkv_rows[:, :, 1]
    values_all = qkv_rows[:, :, 2]
    slopes = alibi_slopes(jnp.arange(H), H)
    scores = masked_scores(queries, keys_all, slopes, doc_ids)
    row_max = lax.optimization_barrier(jnp.max(scores, axis=-1, keepdims=True))
    log_total = row_max + jnp.log(lax.optimization_barrier(jnp.sum(jnp.exp(scores - row_max), axis=-1, keepdims=True)))
    attn_probs = jnp.exp(scores - log_total).astype(jnp.bfloat16)
    context = jnp.einsum('hqk,khe->qhe', attn_probs.astype(jnp.float32), values_all.astype(jnp.float32))
    context = context.astype(jnp.bfloat16).reshape(length, H * HD)
    resid_one = tokens_f + jnp.dot(context, w_dense, preferred_element_type=jnp.float32) + b_dense
    norm_two, normed_two, inv_two = layer_norm(resid_one, ln2_gain, ln2_bias)
    input_two = norm_two.astype(jnp.bfloat16)
    pre_act = jnp.dot(input_two, w_fc1, preferred_element_type=jnp.float32) + b_fc1.reshape(-1)
    hidden = gelu_value(pre_act).astype(jnp.bfloat16)
    block_out = (resid_one + jnp.dot(hidden, w_fc2, preferred_element_type=jnp.float32) + b_fc2).astype(jnp.bfloat16)
    grad_out = cot_row.astype(jnp.float32)
    g_b_fc2 = lax.optimization_barrier(jnp.sum(grad_out, axis=0))
    g_w_fc2 = cross_rows(hidden, cot_row)
    grad_pre = dot_transposed(cot_row, w_fc2) * gelu_slope(pre_act)
    g_b_fc1 = lax.optimization_barrier(jnp.sum(grad_pre, axis=0)).reshape(b_fc1.shape)
    grad_pre_b = grad_pre.astype(jnp.bfloat16)
    g_w_fc1 = cross_rows(input_two, grad_pre_b)
    grad_two = dot_transposed(grad_pre_b, w_fc1)
    grad_ln_two, g_ln2_gain, g_ln2_bias = norm_back(grad_two, normed_two, inv_two, ln2_gain)
    grad_resid = grad_out + grad_ln_two
    g_b_dense = lax.optimization_barrier(jnp.sum(grad_resid, axis=0))
    grad_resid_b = grad_resid.astype(jnp.bfloat16)
    g_w_dense = cross_rows(context, grad_resid_b)
    grad_context = dot_transposed(grad_resid_b, w_dense).reshape(length, H, HD)
    delta = jnp.einsum('qhe,qhe->hq', grad_context, context.reshape(length, H, HD).astype(jnp.float32))
    grad_context_b = grad_context.astype(jnp.bfloat16)
    grad_probs = jnp.einsum('qhe,khe->hqk', grad_context_b.astype(jnp.float32), values_all.astype(jnp.float32))
    prob_full = jnp.exp(scores - log_total)
    grad_scores = (prob_full * (grad_probs - delta[:, :, None])).astype(jnp.bfloat16).astype(jnp.float32)
    inv_root = 1.0 / math.sqrt(HD)
    grad_q = jnp.einsum('hqk,khe->qhe', grad_scores, keys_all.astype(jnp.float32)) * inv_root
    grad_k = jnp.einsum('hqk,qhe->khe', grad_scores, queries.astype(jnp.float32)) * inv_root
    grad_v = jnp.einsum('hqk,qhe->khe', attn_probs.astype(jnp.float32), grad_context_b.astype(jnp.float32))
    g_b_qv = jnp.concatenate([lax.optimization_barrier(jnp.sum(grad_q, axis=0)), lax.optimization_barrier(jnp.sum(grad_v, axis=0))], axis=-1)
    grad_qkv = jnp.stack([grad_q, grad_k, grad_v], axis=2).astype(jnp.bfloat16).reshape(length, 3 * H * HD)
    g_w_qkv = cross_rows(input_one, grad_qkv)
    grad_one = dot_transposed(grad_qkv, w_qkv)
    grad_ln_one, g_ln1_gain, g_ln1_bias = norm_back(grad_one, normed_one, inv_one, ln1_gain)
    d_row = grad_resid + grad_ln_one
    row_grads = (g_ln1_gain, g_ln1_bias, g_w_qkv, g_b_qv, g_w_dense, g_b_dense, g_ln2_gain, g_ln2_bias, g_w_fc1, g_b_fc1, g_w_fc2, g_b_fc2)
    return (block_out, d_row, row_grads)

def reference(tokens, segments, ln1_gain, ln1_bias, w_qkv, b_qv, w_dense, b_dense, ln2_gain, ln2_bias, w_fc1, b_fc1, w_fc2, b_fc2, cotangent):
    weights = (ln1_gain, ln1_bias, w_qkv, b_qv, w_dense, b_dense, ln2_gain, ln2_bias, w_fc1, b_fc1, w_fc2, b_fc2)
    row_total = segments.shape[0]
    length = segments.shape[1]
    tok_rows = tokens.reshape(row_total, length, tokens.shape[1])
    cot_rows = cotangent.reshape(row_total, length, cotangent.shape[1])
    zero_grads = tuple((jnp.zeros(item.shape, jnp.float32) for item in weights))

    def scan_step(carried, inputs):
        tok_row, doc_ids, cot_row = inputs
        out_row, d_row, row_grads = row_pass(weights, tok_row, doc_ids, cot_row)
        summed = tuple((left_val + right_val for left_val, right_val in zip(carried, row_grads)))
        return (summed, (out_row, d_row))
    totals, (out_rows, d_rows) = lax.scan(scan_step, zero_grads, (tok_rows, segments, cot_rows))
    block_out = out_rows.reshape(tokens.shape)
    d_tokens = d_rows.reshape(tokens.shape)
    return (block_out, d_tokens, totals[0], totals[1], totals[2], totals[3], totals[4], totals[5], totals[6], totals[7], totals[8], totals[9], totals[10], totals[11])
```

```python
import functools
import math

import jax
import jax.numpy as jnp
from jax import lax
from jax.experimental import pallas as pl
from jax.experimental.pallas import tpu as pltpu
from jax.sharding import PartitionSpec as P

H = 16


EPS = 1e-05
GELU_C = 0.7978845608028654
GELU_A = 0.044715
MASKED = -1e30


def layer_norm(row_block, gain_row, shift_row):
    row_mean = jnp.mean(row_block, axis=-1, keepdims=True)
    centred = row_block - row_mean
    row_var = jnp.mean(centred * centred, axis=-1, keepdims=True)
    inv_std = lax.rsqrt(row_var + EPS)
    normed = centred * inv_std
    return (normed * gain_row + shift_row, normed, inv_std)


def norm_back(grad_rows, normed, inv_std, gain_row):
    grad_normed = grad_rows * gain_row
    mean_one = jnp.mean(grad_normed, axis=-1, keepdims=True)
    mean_two = jnp.mean(grad_normed * normed, axis=-1, keepdims=True)
    grad_in = inv_std * (grad_normed - mean_one - normed * mean_two)
    return (grad_in, jnp.sum(grad_rows * normed, axis=0), jnp.sum(grad_rows, axis=0))


def gelu_value(pre_act):
    tanh_val = jnp.tanh(GELU_C * (pre_act + GELU_A * pre_act * pre_act * pre_act))
    return 0.5 * pre_act * (1.0 + tanh_val)


def gelu_slope(pre_act):
    tanh_val = jnp.tanh(GELU_C * (pre_act + GELU_A * pre_act * pre_act * pre_act))
    return 0.5 * (1.0 + tanh_val) + 0.5 * pre_act * (1.0 - tanh_val * tanh_val) * GELU_C * (
        1.0 + 3.0 * GELU_A * pre_act * pre_act
    )


def alibi_slopes(head_ids, head_total):
    return jnp.power(2.0, -8.0 * (head_ids.astype(jnp.float32) + 1.0) / head_total)


def qkv_bias(bias_table):
    head_size = bias_table.shape[1] // 2
    zero_keys = jnp.zeros((bias_table.shape[0], head_size), jnp.float32)
    return jnp.concatenate(
        [bias_table[:, :head_size], zero_keys, bias_table[:, head_size:]], axis=1
    ).reshape(-1)


def cross_rows(left_mat, right_mat):
    return lax.dot_general(
        left_mat, right_mat, (((0,), (0,)), ((), ())), preferred_element_type=jnp.float32
    )


def dot_transposed(left_mat, right_mat):
    return lax.dot_general(
        left_mat, right_mat, (((1,), (1,)), ((), ())), preferred_element_type=jnp.float32
    )


def masked_scores(queries, keys_all, slopes, doc_ids, head_size):
    raw_dot = jnp.einsum("qhe,khe->hqk", queries, keys_all, preferred_element_type=jnp.float32)
    places = jnp.arange(doc_ids.shape[0])
    distance = (places[:, None] - places[None, :]).astype(jnp.float32)
    allowed = jnp.logical_and(
        doc_ids[:, None] == doc_ids[None, :], places[None, :] <= places[:, None]
    )
    scores = raw_dot * (1.0 / math.sqrt(head_size)) - slopes[:, None, None] * distance[None]
    return jnp.where(allowed[None], scores, MASKED)


PIECES = 4


def greet(count, me):
    barrier = pltpu.get_barrier_semaphore()
    for step in range(1, count):
        pl.semaphore_signal(
            barrier,
            inc=1,
            device_id={"tensor": lax.rem(me + step, count)},
            device_id_type=pl.DeviceIdType.MESH,
        )
    pl.semaphore_wait(barrier, count - 1)


class Line:
    def __init__(self, count, me, rows, share, stage, landed, sent_sem, got_sem):
        self.count, self.me, self.rows = count, me, rows
        self.size = rows // PIECES
        self.share, self.stage, self.landed = share, stage, landed
        self.sent_sem, self.got_sem = sent_sem, got_sem

    def at(self, piece, chunk):
        return pl.ds(pl.multiple_of(piece * self.rows + chunk * self.size, self.size), self.size)

    def copy(self, way, piece, chunk, source):
        step = 1 if way == 0 else -1
        where = self.at(piece, chunk)
        return pltpu.make_async_remote_copy(
            src_ref=source.at[where],
            dst_ref=self.landed.at[way, where],
            send_sem=self.sent_sem.at[piece, chunk],
            recv_sem=self.got_sem.at[way, piece, chunk],
            device_id={"tensor": self.me + step},
            device_id_type=pl.DeviceIdType.MESH,
        )

    def edges(self, chunk):
        last = self.count - 1

        @pl.when(self.me == 0)
        def _():
            for piece in range(last, 0, -1):
                self.copy(0, piece, chunk, self.share).start()

        @pl.when(self.me == last)
        def _():
            for piece in range(last):
                self.copy(1, piece, chunk, self.share).start()

    def relay_one(self, way, piece, chunk):
        where = self.at(piece, chunk)
        self.copy(way, piece, chunk, self.stage).wait_recv()
        self.stage[where] = (
            self.share[where].astype(jnp.float32) + self.landed[way, where].astype(jnp.float32)
        ).astype(jnp.bfloat16)
        self.copy(way, piece, chunk, self.stage).start()

    def relay(self, chunk):
        last = self.count - 1
        for piece in range(last, 0, -1):
            pl.when(jnp.logical_and(self.me > 0, self.me < piece))(
                functools.partial(self.relay_one, 0, piece, chunk)
            )
            other = last - piece
            pl.when(jnp.logical_and(self.me < last, self.me > other))(
                functools.partial(self.relay_one, 1, other, chunk)
            )

    def total(self, chunk, total_ref):
        where = self.at(self.me, chunk)
        total_ref[...] = self.share[where].astype(jnp.float32)
        for way, there in ((0, self.me > 0), (1, self.me < self.count - 1)):

            @pl.when(there)
            def _(way=way):
                self.copy(way, self.me, chunk, self.stage).wait_recv()
                total_ref[...] += self.landed[way, where].astype(jnp.float32)

        return total_ref[...]

    def finish(self, chunk):
        for piece in range(self.count):

            @pl.when(piece != self.me)
            def _(piece=piece):
                self.copy(0, piece, chunk, self.stage).wait_send()


class Spread:
    def __init__(self, count, me, rows, full, sent_sem, got_sem):
        self.count, self.me, self.rows = count, me, rows
        self.size = rows // PIECES
        self.full, self.sent_sem, self.got_sem = full, sent_sem, got_sem

    def at(self, piece, chunk):
        return pl.ds(pl.multiple_of(piece * self.rows + chunk * self.size, self.size), self.size)

    def copy(self, way, piece, chunk):
        step = 1 if way == 0 else -1
        where = self.at(piece, chunk)
        return pltpu.make_async_remote_copy(
            src_ref=self.full.at[where],
            dst_ref=self.full.at[where],
            send_sem=self.sent_sem.at[way, piece, chunk],
            recv_sem=self.got_sem.at[piece, chunk],
            device_id={"tensor": self.me + step},
            device_id_type=pl.DeviceIdType.MESH,
        )

    def begin(self, chunk, value):
        self.full[self.at(self.me, chunk)] = value

        @pl.when(self.me < self.count - 1)
        def _():
            self.copy(0, self.me, chunk).start()

        @pl.when(self.me > 0)
        def _():
            self.copy(1, self.me, chunk).start()

    def forward_one(self, way, piece, chunk):
        self.copy(way, piece, chunk).wait_recv()

        @pl.when(self.me < self.count - 1 if way == 0 else self.me > 0)
        def _():
            self.copy(way, piece, chunk).start()

    def forward(self, chunk):
        last = self.count - 1
        for piece in range(last, -1, -1):
            pl.when(piece < self.me)(functools.partial(self.forward_one, 0, piece, chunk))
            other = last - piece
            pl.when(other > self.me)(functools.partial(self.forward_one, 1, other, chunk))

    def finish(self, chunk):
        last = self.count - 1
        for piece in range(self.count):

            @pl.when(jnp.logical_and(piece <= self.me, self.me < last))
            def _(piece=piece):
                self.copy(0, piece, chunk).wait_send()

            @pl.when(jnp.logical_and(piece >= self.me, self.me > 0))
            def _(piece=piece):
                self.copy(1, piece, chunk).wait_send()


def each(body, low=0, high=PIECES):
    def step(chunk, carry):
        body(chunk)
        return carry

    lax.fori_loop(low, high, step, 0)


def pipeline(line, spread, final):
    each(line.edges)

    def step(turn):
        pl.when(turn < PIECES)(lambda: line.relay(turn))
        pl.when(jnp.logical_and(turn >= 1, turn <= PIECES))(lambda: final(turn - 1))
        if spread is not None:
            pl.when(turn >= 2)(lambda: spread.forward(turn - 2))

    each(step, 0, PIECES + (1 if spread is None else 2))
    each(line.finish)
    if spread is not None:
        each(spread.finish)


def own(chunk, rows):
    size = rows // PIECES
    return pl.ds(pl.multiple_of(chunk * size, size), size)


def forward_kernel(
    count, share, base, gain, shift, resid, full,
    stage, landed, total, sent, got, spread_sent, spread_got,
):
    me = lax.axis_index("tensor")
    rows = base.shape[0]
    greet(count, me)
    line = Line(count, me, rows, share, stage, landed, sent, got)
    spread = Spread(count, me, rows, full, spread_sent, spread_got)

    def final(chunk):
        where = own(chunk, rows)
        value = base[where] + line.total(chunk, total)
        resid[where] = value
        normed, _, _ = layer_norm(value, gain[...], shift[...])
        spread.begin(chunk, normed.astype(jnp.bfloat16))

    pipeline(line, spread, final)


def middle_kernel(
    count, share, resid, grads, gain, grad_resid, sums, full,
    stage, landed, total, sent, got, spread_sent, spread_got,
):
    me = lax.axis_index("tensor")
    rows = resid.shape[0]
    greet(count, me)
    line = Line(count, me, rows, share, stage, landed, sent, got)
    spread = Spread(count, me, rows, full, spread_sent, spread_got)
    sums[...] = jnp.zeros_like(sums)

    def final(chunk):
        where = own(chunk, rows)
        grad_two = line.total(chunk, total)
        _, normed, inv = layer_norm(resid[where], gain[...], gain[...])
        grad_in, sum_gain, sum_shift = norm_back(grad_two, normed, inv, gain[...])
        grad_own = grads[where].astype(jnp.float32)
        value = grad_own + grad_in
        grad_resid[where] = value
        spread.begin(chunk, value.astype(jnp.bfloat16))
        sums[0:1] += sum_gain[None]
        sums[1:2] += sum_shift[None]
        sums[2:3] += jnp.sum(value, axis=0, keepdims=True)
        sums[3:4] += jnp.sum(grad_own, axis=0, keepdims=True)

    pipeline(line, spread, final)


def last_kernel(
    count, share, rows_in, grad_resid, early, gain, d_tokens, sums_out,
    stage, landed, total, sums, others, sent, got, sum_sent, sum_got,
):
    me = lax.axis_index("tensor")
    rows = rows_in.shape[0]
    greet(count, me)
    line = Line(count, me, rows, share, stage, landed, sent, got)
    sums[...] = early[...]

    def final(chunk):
        where = own(chunk, rows)
        grad_one = line.total(chunk, total)
        _, normed, inv = layer_norm(rows_in[where].astype(jnp.float32), gain[...], gain[...])
        grad_in, sum_gain, sum_shift = norm_back(grad_one, normed, inv, gain[...])
        d_tokens[where] = grad_resid[where] + grad_in
        sums[4:5] += sum_gain[None]
        sums[5:6] += sum_shift[None]

    pipeline(line, None, final)
    copies = []
    for step in range(1, count):
        copies.append(
            pltpu.make_async_remote_copy(
                src_ref=sums,
                dst_ref=others.at[step],
                send_sem=sum_sent.at[step],
                recv_sem=sum_got.at[step],
                device_id={"tensor": lax.rem(me + step, count)},
                device_id_type=pl.DeviceIdType.MESH,
            )
        )
    for copy in copies:
        copy.start()
    for copy in copies:
        copy.wait()
    value = sums[...]
    for step in range(1, count):
        value = value + others[step]
    sums_out[...] = value


def call(kernel, ident, count, operands, outs, spreads, sums):
    length, width = operands[0].shape
    scratch = [
        pltpu.VMEM((length, width), jnp.bfloat16),
        pltpu.VMEM((2, length, width), jnp.bfloat16),
        pltpu.VMEM((length // count // PIECES, width), jnp.float32),
    ]
    if sums:
        scratch += [
            pltpu.VMEM((8, width), jnp.float32),
            pltpu.VMEM((count, 8, width), jnp.float32),
        ]
    scratch += [
        pltpu.SemaphoreType.DMA((count, PIECES)),
        pltpu.SemaphoreType.DMA((2, count, PIECES)),
    ]
    if spreads:
        scratch += [
            pltpu.SemaphoreType.DMA((2, count, PIECES)),
            pltpu.SemaphoreType.DMA((count, PIECES)),
        ]
    if sums:
        scratch += [pltpu.SemaphoreType.DMA((count,)), pltpu.SemaphoreType.DMA((count,))]
    vmem = pl.BlockSpec(memory_space=pltpu.VMEM)
    return pl.pallas_call(
        functools.partial(kernel, count),
        out_shape=[jax.ShapeDtypeStruct(shape, dtype) for shape, dtype in outs],
        in_specs=[vmem] * len(operands),
        out_specs=[vmem] * len(outs),
        scratch_shapes=scratch,
        compiler_params=pltpu.CompilerParams(
            collective_id=ident, has_side_effects=True, vmem_limit_bytes=24 << 20
        ),
        cost_estimate=pl.CostEstimate(
            flops=length * width * 20, bytes_accessed=length * width * 64, transcendentals=0
        ),
    )(*operands)


def local(
    tokens,
    segments,
    ln1_gain,
    ln1_bias,
    w_qkv,
    b_qv,
    w_dense,
    b_dense,
    ln2_gain,
    ln2_bias,
    w_fc1,
    b_fc1,
    w_fc2,
    b_fc2,
    cotangent,
):
    tensor_count = lax.axis_size("tensor")
    tensor_rank = lax.axis_index("tensor")
    length = tokens.shape[0]
    share_rows = length // tensor_count
    head_count = b_qv.shape[0]
    head_size = b_qv.shape[1] // 2
    offset = tensor_rank * share_rows
    doc_ids = segments[0]
    tokens_f = tokens.astype(jnp.float32)
    norm_one, normed_one, inv_one = layer_norm(tokens_f, ln1_gain, ln1_bias)
    input_one = norm_one.astype(jnp.bfloat16)
    qkv_rows = (
        jnp.dot(input_one, w_qkv, preferred_element_type=jnp.float32) + qkv_bias(b_qv)
    ).astype(jnp.bfloat16)
    qkv_rows = qkv_rows.reshape(length, head_count, 3, head_size)
    queries = qkv_rows[:, :, 0]
    keys_all = qkv_rows[:, :, 1]
    values_all = qkv_rows[:, :, 2]
    slopes = alibi_slopes(tensor_rank * head_count + jnp.arange(head_count), H)
    scores = masked_scores(queries, keys_all, slopes, doc_ids, head_size)
    row_max = jnp.max(scores, axis=-1, keepdims=True)
    log_total = row_max + jnp.log(jnp.sum(jnp.exp(scores - row_max), axis=-1, keepdims=True))
    attn_probs = jnp.exp(scores - log_total).astype(jnp.bfloat16)
    context = jnp.einsum("hqk,khe->qhe", attn_probs, values_all, preferred_element_type=jnp.float32)
    context = context.astype(jnp.bfloat16).reshape(length, head_count * head_size)
    width = tokens.shape[1]
    own_tokens = lax.dynamic_slice_in_dim(tokens, offset, share_rows, 0)
    resid_one, input_two = call(
        forward_kernel,
        1,
        tensor_count,
        (
            jnp.dot(context, w_dense, preferred_element_type=jnp.float32).astype(jnp.bfloat16),
            own_tokens.astype(jnp.float32) + b_dense,
            ln2_gain[None],
            ln2_bias[None],
        ),
        (((share_rows, width), jnp.float32), ((length, width), jnp.bfloat16)),
        True,
        False,
    )
    pre_act = jnp.dot(input_two, w_fc1, preferred_element_type=jnp.float32) + b_fc1.reshape(-1)
    hidden = gelu_value(pre_act).astype(jnp.bfloat16)
    mlp_share = lax.psum_scatter(
        jnp.dot(hidden, w_fc2, preferred_element_type=jnp.float32).astype(jnp.bfloat16),
        "tensor",
        scatter_dimension=0,
        tiled=True,
    ).astype(jnp.float32)
    block_out = (resid_one + mlp_share + b_fc2).astype(jnp.bfloat16)
    grad_share = lax.dynamic_slice_in_dim(cotangent, offset, share_rows, 0)
    g_w_fc2 = cross_rows(hidden, cotangent)
    grad_pre = dot_transposed(cotangent, w_fc2) * gelu_slope(pre_act)
    g_b_fc1 = jnp.sum(grad_pre, axis=0).reshape(b_fc1.shape)
    grad_pre_b = grad_pre.astype(jnp.bfloat16)
    g_w_fc1 = cross_rows(input_two, grad_pre_b)
    grad_resid, sums_two, grad_resid_b = call(
        middle_kernel,
        2,
        tensor_count,
        (
            dot_transposed(grad_pre_b, w_fc1).astype(jnp.bfloat16),
            resid_one,
            grad_share,
            ln2_gain[None],
        ),
        (
            ((share_rows, width), jnp.float32),
            ((8, width), jnp.float32),
            ((length, width), jnp.bfloat16),
        ),
        True,
        False,
    )
    g_w_dense = cross_rows(context, grad_resid_b)
    grad_context = dot_transposed(grad_resid_b, w_dense).reshape(length, head_count, head_size)
    delta = jnp.einsum(
        "qhe,qhe->hq",
        grad_context,
        context.reshape(length, head_count, head_size).astype(jnp.float32),
    )
    grad_context_b = grad_context.astype(jnp.bfloat16)
    grad_probs = jnp.einsum(
        "qhe,khe->hqk", grad_context_b, values_all, preferred_element_type=jnp.float32
    )
    again_scores = masked_scores(queries, keys_all, slopes, doc_ids, head_size)
    prob_full = jnp.exp(again_scores - log_total)
    again_probs = prob_full.astype(jnp.bfloat16)
    grad_scores = (prob_full * (grad_probs - delta[:, :, None])).astype(jnp.bfloat16)
    inv_root = 1.0 / math.sqrt(head_size)
    grad_q = (
        jnp.einsum("hqk,khe->qhe", grad_scores, keys_all, preferred_element_type=jnp.float32)
        * inv_root
    )
    grad_k = (
        jnp.einsum("hqk,qhe->khe", grad_scores, queries, preferred_element_type=jnp.float32)
        * inv_root
    )
    grad_v = jnp.einsum(
        "hqk,qhe->khe", again_probs, grad_context_b, preferred_element_type=jnp.float32
    )
    g_b_qv = jnp.concatenate([jnp.sum(grad_q, axis=0), jnp.sum(grad_v, axis=0)], axis=-1)
    grad_qkv = (
        jnp.stack([grad_q, grad_k, grad_v], axis=2)
        .astype(jnp.bfloat16)
        .reshape(length, 3 * head_count * head_size)
    )
    g_w_qkv = cross_rows(input_one, grad_qkv)
    d_tokens, sums_all = call(
        last_kernel,
        3,
        tensor_count,
        (
            dot_transposed(grad_qkv, w_qkv).astype(jnp.bfloat16),
            own_tokens,
            grad_resid,
            sums_two,
            ln1_gain[None],
        ),
        (((share_rows, width), jnp.float32), ((8, width), jnp.float32)),
        False,
        True,
    )
    dp_count = lax.axis_size("dp")

    def scatter(grad, dim):
        return lax.psum_scatter(
            grad.astype(jnp.bfloat16), "dp", scatter_dimension=dim, tiled=True
        ).astype(jnp.float32)

    sent_fc2 = scatter(g_w_fc2, 1)
    sent_fc1 = scatter(g_w_fc1, 0)
    sent_dense = scatter(g_w_dense, 1)
    sent_qkv = scatter(g_w_qkv, 0)
    split = width // (dp_count * tensor_count)
    gains = lax.dynamic_index_in_dim(
        sums_all[:6].reshape(6, dp_count, tensor_count, split), tensor_rank, 2, keepdims=False
    )
    qv_rows, qv_cols = g_b_qv.shape[0], g_b_qv.shape[1] // dp_count
    up_rows, up_cols = g_b_fc1.shape[0], g_b_fc1.shape[1] // dp_count
    packed = jnp.concatenate(
        [
            jnp.moveaxis(gains, 1, 0).reshape(dp_count, -1),
            jnp.moveaxis(g_b_qv.reshape(qv_rows, dp_count, qv_cols), 1, 0).reshape(dp_count, -1),
            jnp.moveaxis(g_b_fc1.reshape(up_rows, dp_count, up_cols), 1, 0).reshape(dp_count, -1),
        ],
        axis=1,
    )
    small = lax.psum_scatter(packed, "dp", scatter_dimension=0, tiled=True)[0]
    gain_sums = small[: 6 * split].reshape(6, split)
    sent_qv = small[6 * split : 6 * split + qv_rows * qv_cols].reshape(qv_rows, qv_cols)
    sent_bias = small[6 * split + qv_rows * qv_cols :].reshape(up_rows, up_cols)
    small_sums = (
        gain_sums[4],
        gain_sums[5],
        gain_sums[2],
        gain_sums[0],
        gain_sums[1],
        gain_sums[3],
    )
    return (
        block_out,
        d_tokens,
        small_sums[0],
        small_sums[1],
        sent_qkv,
        sent_qv,
        sent_dense,
        small_sums[2],
        small_sums[3],
        small_sums[4],
        sent_fc1,
        sent_bias,
        sent_fc2,
        small_sums[5],
    )


def solution(mesh):
    placed = (
        P("dp", None),
        P("dp", None),
        P(),
        P(),
        P(None, "tensor"),
        P("tensor", None),
        P("tensor", None),
        P(),
        P(),
        P(),
        P(None, "tensor"),
        P("tensor", None),
        P("tensor", None),
        P(),
        P("dp", None),
    )
    return jax.shard_map(
        local,
        mesh=mesh,
        in_specs=placed,
        out_specs=(
            P(("dp", "tensor"), None),
            P(("dp", "tensor"), None),
            P(("dp", "tensor")),
            P(("dp", "tensor")),
            P("dp", "tensor"),
            P("tensor", "dp"),
            P("tensor", "dp"),
            P(("dp", "tensor")),
            P(("dp", "tensor")),
            P(("dp", "tensor")),
            P("dp", "tensor"),
            P("tensor", "dp"),
            P("tensor", "dp"),
            P(("dp", "tensor")),
        ),
        check_vma=False,
    )
```
